512 devices in a mesh: site: 32 (over x_lo, z), sector: 16 (over y, x_hi, core).
Axes of the slice: x: 4 (x_hi: 2, x_lo: 2; x = x_hi * 2 + x_lo), y: 4, z: 16, core: 2. Of those that a mesh axis runs over, the one named last changes fastest.
Arguments:
- site_tensors: bfloat16 [32, 2, 6144, 384], P('site', None, 'sector'), may hold values from -0.21875 to 0.21875
- environments: bfloat16 [32, 5, 6144, 384], P('site', None, 'sector'), may hold values from -6 to 6
- mpo: float32 [32, 5, 5, 2, 2], P('site'), may hold values from -4 to 4
- boundary: bfloat16 [5, 6144, 384], P(None, 'sector'), may hold values from -6 to 6
Outputs:
- environments_out: bfloat16 [32, 5, 6144, 384], P('site', None, 'sector')
The draws below stay inside these ranges and needn't reach their ends.
All inputs are finite; a program needn't handle non-finite values.
Results may differ from the reference program's by a relative error of at most 0.0054.
Values may be sent and summed in bfloat16 or wider, within the bound.
No kernel may reach another device: no remote copies, remote signals or barrier semaphores. Data moves between devices by JAX's collectives and lax.ppermute only.
A program may use at most 64 MiB of HBM per device.

```python
import jax
import jax.numpy as jnp
import numpy as np
from jax import lax

SEC = 384
W = 5
TICKS = 1
NSEC = 16
CHI = 6144
SITES = 32


def block_levels(key, shape, shards, low, largest):
    factor_of, own = 1.0, jax.random.fold_in(key, 6)
    for dim, shards_of in shards:
        draws = jnp.exp(jax.random.uniform(jax.random.fold_in(own, dim), (shards_of,), jnp.float32, low / len(shards), largest / len(shards)))
        factor_of = factor_of * jnp.repeat(draws, shape[dim] // shards_of).reshape([-1 if axis == dim else 1 for axis in range(len(shape))])
    return factor_of


def normal_values(rng, shape, spread, bound, pieces=(), kind=jnp.bfloat16):
    values = spread * jax.random.normal(rng, shape, jnp.float32)
    if pieces:
        values = values * block_levels(rng, shape, pieces, -0.22, 0.18)
    return jnp.clip(values, -bound, bound).astype(kind)


def setup_inputs(seed: int = 0) -> dict:
    key_list = jax.random.split(jax.random.key(seed), 5)
    return {
        "site_tensors": normal_values(key_list[0], (SITES, 2, CHI, SEC), (2 * SEC) ** -0.5, 0.21875, ((0, 32), (2, 16))),
        "environments": normal_values(key_list[1], (SITES, W, CHI, SEC), 1.0, 6.0, ((0, 32), (2, 16))),
        "mpo": normal_values(key_list[2], (SITES, W, W, 2, 2), 0.6, 4.0, ((0, 32),), jnp.float32),
        "boundary": normal_values(key_list[3], (W, CHI, SEC), 1.0, 6.0, ((1, 16),)),
    }


charge_steps = (0, 1, -1, 0, 0)


def allowed():
    charges = np.array(charge_steps)
    spins = np.arange(2)
    differ = charges[None, :] - charges[:, None]
    return (spins[None, None, None, :] - spins[None, None, :, None] == differ[:, :, None, None]).astype(np.float32)


def transfer(incoming, blocks, weights):
    env_blocks = incoming.reshape(W, NSEC, SEC, SEC).astype(jnp.float32)
    site_blocks = blocks.reshape(2, NSEC, SEC, SEC).astype(jnp.float32)
    rolled = jnp.stack([jnp.roll(site_blocks, -charge_steps[term], axis=1) for term in range(W)])
    products = jnp.einsum('wqab,wtqbc->wtqac', env_blocks, rolled)
    couplings = weights * jnp.asarray(allowed(), weights.dtype)
    combined = jnp.einsum('wvst,wtqac->vsqac', couplings, products, precision=lax.Precision.HIGHEST).astype(jnp.bfloat16)
    halves = jnp.einsum('sqba,vsqbc->vsqac', site_blocks, combined.astype(jnp.float32))
    carried = lax.optimization_barrier(halves[:, 1].astype(jnp.bfloat16))
    carried = jnp.roll(carried.astype(jnp.float32), 1, axis=1)
    updated = (halves[:, 0] + carried).astype(jnp.bfloat16)
    return updated.reshape(W, CHI, SEC)


def reference(site_tensors, environments, mpo, boundary):
    state = environments
    for tick_index in range(TICKS):
        incoming = jnp.concatenate([boundary[None], state[:-1]], axis=0)
        state = lax.map(lambda item: transfer(item[0], item[1], item[2]), (incoming, site_tensors, mpo))
    return state
```

```python
import jax
import jax.numpy as jnp
from jax import lax
from jax.experimental import pallas as pl
from jax.experimental.pallas import tpu as pltpu
from jax.sharding import PartitionSpec as P


BF16 = jnp.bfloat16
F32 = jnp.float32
AXES = ("site", "sector")
FLAT = (0, 3, 4)
ROWS = 128
VMEM = 24 * 2**20


def dot(a, b):
    return jnp.dot(a, b, preferred_element_type=F32)


def row_blocks(count):
    step = ROWS if count % ROWS == 0 else count
    return [slice(start, start + step) for start in range(0, count, step)]


def coupling(ref, w, v, s, t):
    return ref[w * 20 + v * 4 + s * 2 + t]


def whole():
    return pl.BlockSpec(memory_space=pltpu.VMEM)


def scalars():
    return pl.BlockSpec(memory_space=pltpu.SMEM)


def kernel_call(body, outs, flops, specs, scratch=()):
    return pl.pallas_call(
        body,
        out_shape=[jax.ShapeDtypeStruct(shape, kind) for shape, kind in outs],
        in_specs=specs,
        out_specs=[whole() for _ in outs],
        scratch_shapes=list(scratch),
        cost_estimate=pl.CostEstimate(flops=flops, bytes_accessed=4_000_000, transcendentals=0),
        compiler_params=pltpu.CompilerParams(vmem_limit_bytes=VMEM),
    )


def early(k, bnd, arr, own, near, up, z034, z1, c2, own_t, near_t, y):
    first = lax.axis_index("site") == 0
    e0 = jnp.where(first, bnd[0], arr[0])
    e1 = jnp.where(first, bnd[1], arr[1])
    own_t[0] = own[0].T
    own_t[1] = own[1].T
    near_t[...] = near[1].T
    y[0] = dot(e0, own[0])
    y[1] = dot(e0, own[1])
    y[2] = dot(e1, up[...])
    for r in row_blocks(y.shape[1]):
        for i, v in enumerate(FLAT):
            z034[i, r] = coupling(k, 0, v, 0, 0) * y[0, r]
        c2[r] = coupling(k, 0, 2, 1, 0) * y[0, r]
        z1[r] = coupling(k, 0, 1, 0, 1) * y[1, r] + coupling(k, 1, 1, 0, 0) * y[2, r]


def middle(k, bnd, arr34, arr10, got10, own, own_t, near, near_t, z034_in, z1_in, c2_in,
           z034, c2, m034, out1, y):
    first = lax.axis_index("site") == 0
    e3 = jnp.where(first, bnd[3], arr34[0])
    e4 = jnp.where(first, bnd[4], arr34[1])
    f0 = jnp.where(first, arr10[0], got10[0])
    f1 = jnp.where(first, arr10[1], got10[1])
    y[0] = dot(e3, own[0])
    y[1] = dot(e3, own[1])
    y[2] = dot(e4, own[0])
    y[3] = dot(e4, own[1])
    y[4] = dot(f0, near[1])
    y[5] = dot(f1, own[0])
    y[6] = dot(f1, own[1])
    z1 = []
    m1 = []
    for r in row_blocks(y.shape[1]):
        for i, v in enumerate(FLAT):
            z034[i, r] = (
                z034_in[i, r]
                + coupling(k, 3, v, 0, 0) * y[0, r]
                + coupling(k, 4, v, 0, 0) * y[2, r]
            )
            m034[i, r] = coupling(k, 0, v, 1, 1) * y[4, r] + coupling(k, 1, v, 1, 0) * y[5, r]
        c2[r] = c2_in[r] + coupling(k, 3, 2, 1, 0) * y[0, r] + coupling(k, 4, 2, 1, 0) * y[2, r]
        z1.append(
            (
                z1_in[r] + coupling(k, 3, 1, 0, 1) * y[1, r] + coupling(k, 4, 1, 0, 1) * y[3, r]
            ).astype(BF16)
        )
        m1.append((coupling(k, 1, 1, 1, 1) * y[6, r]).astype(BF16))
    carried = dot(near_t[...], jnp.concatenate(m1, axis=0)).astype(BF16)
    out1[...] = (dot(own_t[0], jnp.concatenate(z1, axis=0)) + carried.astype(F32)).astype(BF16)


def send(k, bnd, arr2, near, own_t, c2_in, c2, y2):
    e2 = jnp.where(lax.axis_index("site") == 0, bnd[2], arr2[0])
    y2[...] = dot(e2, near[1])
    z = (c2_in[...] + coupling(k, 2, 2, 1, 1) * y2[...]).astype(BF16)
    c2[...] = dot(own_t[1], z).astype(BF16)


def late(k, bnd, arr2, near, own_t, z034_in, y2, p0, last):
    e2 = jnp.where(lax.axis_index("site") == 0, bnd[2], arr2[0])
    y = dot(e2, near[0])
    last[...] = dot(own_t[0], (coupling(k, 2, 2, 0, 0) * y).astype(BF16))
    for i, v in enumerate(FLAT):
        z = (z034_in[i] + coupling(k, 2, v, 0, 1) * y2[...]).astype(BF16)
        p0[i] = dot(own_t[0], z)


def join(k, arr34, got34, near, near_t, m034, p0, out1, out, y):
    first = lax.axis_index("site") == 0
    y[0] = dot(jnp.where(first, arr34[0], got34[0]), near[1])
    y[1] = dot(jnp.where(first, arr34[1], got34[1]), near[1])
    out[0, 1] = out1[...]
    for i, v in enumerate(FLAT):
        z = (
            m034[i] + coupling(k, 3, v, 1, 1) * y[0] + coupling(k, 4, v, 1, 1) * y[1]
        ).astype(BF16)
        carried = dot(near_t[...], z).astype(BF16)
        out[0, v] = (p0[i] + carried.astype(F32)).astype(BF16)


def finish(out_in, p0, c2, out, buf, sem):
    buf[...] = (p0[...] + c2[...].astype(F32)).astype(BF16)
    copy = pltpu.make_async_copy(buf, out.at[0, 2], sem)
    copy.start()
    copy.wait()


def local(sites, sectors, site_tensors, environments, mpo, boundary):
    def pairs(move, starts):
        found = []
        for s in starts:
            for q in range(sectors):
                to, r = move(s, q)
                found.append((s * sectors + q, to * sectors + r % sectors))
        return found

    everywhere = range(sites)
    ahead = pairs(lambda s, q: (s, q + 1), everywhere)
    behind = pairs(lambda s, q: (s, q - 1), everywhere)
    inner = pairs(lambda s, q: (s, q + 1), range(1, sites))
    along = pairs(lambda s, q: (s + 1, q) if s + 1 < sites else (0, q + 1), everywhere)
    along_open = pairs(lambda s, q: (s + 1, q), range(sites - 1))

    own = site_tensors[0]
    env = environments[0]
    size = own.shape[-1]
    block = (size, size)
    flop = 2 * size**3
    k = mpo.reshape(-1)
    last = lax.axis_index("site") == sites - 1

    def send_on(value, route):
        return lax.ppermute(value, AXES, route)

    first_piece = jnp.where(last, boundary[0:2], env[0:2])
    arr10 = send_on(first_piece, along)
    near = send_on(own, ahead)
    env_later, _ = lax.optimization_barrier((env, first_piece))
    arr34 = send_on(jnp.where(last, boundary[3:5], env_later[3:5]), along)
    up = send_on(own[0], behind)
    arr2 = send_on(env_later[2:3], along_open)
    got10 = send_on(arr10, inner)

    v = whole()
    z034, z1, c2, own_t, near_t = kernel_call(
        early,
        [((3, *block), F32), (block, F32), (block, F32), ((2, *block), BF16), (block, BF16)],
        3 * flop,
        [scalars()] + [v] * 5,
        [pltpu.VMEM((3, *block), F32)],
    )(k, boundary, arr10, own, near, up)
    got34 = send_on(arr34, inner)
    z034, c2, m034, out1 = kernel_call(
        middle,
        [((3, *block), F32), (block, F32), ((3, *block), F32), (block, BF16)],
        9 * flop,
        [scalars()] + [v] * 11,
        [pltpu.VMEM((7, *block), F32)],
    )(k, boundary, arr34, arr10, got10, own, own_t, near, near_t, z034, z1, c2)
    c2, y2 = kernel_call(
        send, [(block, BF16), (block, F32)], 2 * flop, [scalars()] + [v] * 5
    )(k, boundary, arr2, near, own_t, c2)
    c2 = send_on(c2, ahead)
    p0, tail = kernel_call(
        late, [((3, *block), F32), (block, F32)], 5 * flop, [scalars()] + [v] * 6
    )(k, boundary, arr2, near, own_t, z034, y2)
    (out,) = kernel_call(
        join,
        [((1, 5, *block), BF16)],
        5 * flop,
        [scalars()] + [v] * 7,
        [pltpu.VMEM((2, *block), F32)],
    )(k, arr34, got34, near, near_t, m034, p0, out1)
    (out,) = pl.pallas_call(
        finish,
        out_shape=[jax.ShapeDtypeStruct((1, 5, *block), BF16)],
        in_specs=[pl.BlockSpec(memory_space=pl.ANY), v, v],
        out_specs=[pl.BlockSpec(memory_space=pl.ANY)],
        scratch_shapes=[pltpu.VMEM(block, BF16), pltpu.SemaphoreType.DMA],
        input_output_aliases={0: 0},
        cost_estimate=pl.CostEstimate(flops=size * size, bytes_accessed=1_000_000, transcendentals=0),
        compiler_params=pltpu.CompilerParams(vmem_limit_bytes=VMEM),
        name="finish",
    )(out, tail, c2)
    return out


def solution(mesh):
    in_specs = (
        P("site", None, "sector", None),
        P("site", None, "sector", None),
        P("site", None, None, None, None),
        P(None, "sector", None),
    )

    def body(*args):
        return local(mesh.shape["site"], mesh.shape["sector"], *args)

    return jax.shard_map(
        body, mesh=mesh, in_specs=in_specs, out_specs=P("site", None, "sector", None), check_vma=False
    )
```

```python
import jax
import jax.numpy as jnp
from jax import lax
from jax.experimental import pallas as pl
from jax.experimental.pallas import tpu as pltpu
from jax.sharding import PartitionSpec as P


BF16 = jnp.bfloat16
F32 = jnp.float32
AXES = ("site", "sector")
FLAT = (0, 3, 4)
ROWS = 128
VMEM = 24 * 2**20


def dot(a, b):
    return jnp.dot(a, b, preferred_element_type=F32)


def row_blocks(count):
    step = ROWS if count % ROWS == 0 else count
    return [slice(start, start + step) for start in range(0, count, step)]


def coupling(ref, w, v, s, t):
    return ref[w * 20 + v * 4 + s * 2 + t]


def whole():
    return pl.BlockSpec(memory_space=pltpu.VMEM)


def scalars():
    return pl.BlockSpec(memory_space=pltpu.SMEM)


def kernel_call(body, outs, flops, specs, scratch=()):
    return pl.pallas_call(
        body,
        out_shape=[jax.ShapeDtypeStruct(shape, kind) for shape, kind in outs],
        in_specs=specs,
        out_specs=[whole() for _ in outs],
        scratch_shapes=list(scratch),
        cost_estimate=pl.CostEstimate(flops=flops, bytes_accessed=4_000_000, transcendentals=0),
        compiler_params=pltpu.CompilerParams(vmem_limit_bytes=VMEM),
    )


def split(env, bnd, own, s34, s2, own_up):
    s34[...] = jnp.where(
        lax.axis_index("site") == lax.axis_size("site") - 1, bnd[3:5], env[3:5]
    )
    s2[...] = env[2:3]
    own_up[...] = own[0]


def early(k, bnd, arr, own, z034, z1, c2, own_t, y):
    first = lax.axis_index("site") == 0
    e0 = jnp.where(first, bnd[0], arr[0])
    own_t[0] = own[0].T
    own_t[1] = own[1].T
    y[0] = dot(e0, own[0])
    y[1] = dot(e0, own[1])
    for r in row_blocks(y.shape[1]):
        for i, v in enumerate(FLAT):
            z034[i, r] = coupling(k, 0, v, 0, 0) * y[0, r]
        c2[r] = coupling(k, 0, 2, 1, 0) * y[0, r]
        z1[r] = coupling(k, 0, 1, 0, 1) * y[1, r]


def middle(k, bnd, arr34, arr10, got10, own, near, z034_in, z1_in, c2_in,
           z034, z1, c2, m034, carried1, near_t, y):
    first = lax.axis_index("site") == 0
    e3 = jnp.where(first, bnd[3], arr34[0])
    e4 = jnp.where(first, bnd[4], arr34[1])
    f0 = jnp.where(first, arr10[0], got10[0])
    f1 = jnp.where(first, arr10[1], got10[1])
    y[0] = dot(e3, own[0])
    y[1] = dot(e3, own[1])
    y[2] = dot(e4, own[0])
    y[3] = dot(e4, own[1])
    y[4] = dot(f0, near[1])
    y[5] = dot(f1, own[0])
    y[6] = dot(f1, own[1])
    m1 = []
    near_t[...] = near[1].T
    for r in row_blocks(y.shape[1]):
        for i, v in enumerate(FLAT):
            z034[i, r] = (
                z034_in[i, r]
                + coupling(k, 3, v, 0, 0) * y[0, r]
                + coupling(k, 4, v, 0, 0) * y[2, r]
            )
            m034[i, r] = coupling(k, 0, v, 1, 1) * y[4, r] + coupling(k, 1, v, 1, 0) * y[5, r]
        c2[r] = c2_in[r] + coupling(k, 3, 2, 1, 0) * y[0, r] + coupling(k, 4, 2, 1, 0) * y[2, r]
        z1[r] = z1_in[r] + coupling(k, 3, 1, 0, 1) * y[1, r] + coupling(k, 4, 1, 0, 1) * y[3, r]
        m1.append((coupling(k, 1, 1, 1, 1) * y[6, r]).astype(BF16))
    carried1[...] = dot(near_t[...], jnp.concatenate(m1, axis=0)).astype(BF16)


def send(k, bnd, arr2, near, own_t, c2_in, c2, y2):
    e2 = jnp.where(lax.axis_index("site") == 0, bnd[2], arr2[0])
    y2[...] = dot(e2, near[1])
    z = (c2_in[...] + coupling(k, 2, 2, 1, 1) * y2[...]).astype(BF16)
    c2[...] = dot(own_t[1], z).astype(BF16)


def late(k, bnd, arr2, arr10, near, up, own_t, z034_in, z1_in, carried1, y2, p0, last, out1):
    e2 = jnp.where(lax.axis_index("site") == 0, bnd[2], arr2[0])
    y = dot(e2, near[0])
    last[...] = dot(own_t[0], (coupling(k, 2, 2, 0, 0) * y).astype(BF16))
    for i, v in enumerate(FLAT):
        z = (z034_in[i] + coupling(k, 2, v, 0, 1) * y2[...]).astype(BF16)
        p0[i] = dot(own_t[0], z)
    e1 = jnp.where(lax.axis_index("site") == 0, bnd[1], arr10[1])
    y = dot(e1, up[...])
    z = (z1_in[...] + coupling(k, 1, 1, 0, 0) * y).astype(BF16)
    out1[...] = (dot(own_t[0], z) + carried1[...].astype(F32)).astype(BF16)


def join(k, arr34, got34, near, near_t, m034, p0, out1, out, y):
    first = lax.axis_index("site") == 0
    y[0] = dot(jnp.where(first, arr34[0], got34[0]), near[1])
    y[1] = dot(jnp.where(first, arr34[1], got34[1]), near[1])
    out[0, 1] = out1[...]
    for i, v in enumerate(FLAT):
        z = (
            m034[i] + coupling(k, 3, v, 1, 1) * y[0] + coupling(k, 4, v, 1, 1) * y[1]
        ).astype(BF16)
        carried = dot(near_t[...], z).astype(BF16)
        out[0, v] = (p0[i] + carried.astype(F32)).astype(BF16)


def finish(out_in, p0, c2, out, buf, sem):
    buf[...] = (p0[...] + c2[...].astype(F32)).astype(BF16)
    copy = pltpu.make_async_copy(buf, out.at[0, 2], sem)
    copy.start()
    copy.wait()


def local(sites, sectors, site_tensors, environments, mpo, boundary):
    def pairs(move, starts):
        found = []
        for s in starts:
            for q in range(sectors):
                to, r = move(s, q)
                found.append((s * sectors + q, to * sectors + r % sectors))
        return found

    everywhere = range(sites)
    ahead = pairs(lambda s, q: (s, q + 1), everywhere)
    behind = pairs(lambda s, q: (s, q - 1), everywhere)
    inner = pairs(lambda s, q: (s, q + 1), range(1, sites))
    along = pairs(lambda s, q: (s + 1, q) if s + 1 < sites else (0, q + 1), everywhere)
    along_open = pairs(lambda s, q: (s + 1, q), range(sites - 1))

    own = site_tensors[0]
    env = environments[0]
    size = own.shape[-1]
    block = (size, size)
    flop = 2 * size**3
    k = mpo.reshape(-1)
    last = lax.axis_index("site") == sites - 1

    def send_on(value, route):
        return lax.ppermute(value, AXES, route)

    v = whole()
    arr10 = send_on(jnp.where(last, boundary[0:2], env[0:2]), along)
    s34, s2, own_up = kernel_call(
        split, [((2, *block), BF16), ((1, *block), BF16), (block, BF16)], size * size, [v] * 3
    )(env, boundary, own)
    near = send_on(own, ahead)
    arr34 = send_on(s34, along)
    up = send_on(own_up, behind)
    arr2 = send_on(s2, along_open)
    got10 = send_on(arr10, inner)

    z034, z1, c2, own_t = kernel_call(
        early,
        [((3, *block), F32), (block, F32), (block, F32), ((2, *block), BF16)],
        2 * flop,
        [scalars()] + [v] * 3,
        [pltpu.VMEM((2, *block), F32)],
    )(k, boundary, arr10, own)
    got34 = send_on(arr34, inner)
    z034, z1, c2, m034, carried1, near_t = kernel_call(
        middle,
        [
            ((3, *block), F32),
            (block, F32),
            (block, F32),
            ((3, *block), F32),
            (block, BF16),
            (block, BF16),
        ],
        8 * flop,
        [scalars()] + [v] * 9,
        [pltpu.VMEM((7, *block), F32)],
    )(k, boundary, arr34, arr10, got10, own, near, z034, z1, c2)
    c2, y2 = kernel_call(
        send, [(block, BF16), (block, F32)], 2 * flop, [scalars()] + [v] * 5
    )(k, boundary, arr2, near, own_t, c2)
    c2 = send_on(c2, ahead)
    p0, tail, out1 = kernel_call(
        late, [((3, *block), F32), (block, F32), (block, BF16)], 7 * flop, [scalars()] + [v] * 10
    )(k, boundary, arr2, arr10, near, up, own_t, z034, z1, carried1, y2)
    (out,) = kernel_call(
        join,
        [((1, 5, *block), BF16)],
        5 * flop,
        [scalars()] + [v] * 7,
        [pltpu.VMEM((2, *block), F32)],
    )(k, arr34, got34, near, near_t, m034, p0, out1)
    (out,) = pl.pallas_call(
        finish,
        out_shape=[jax.ShapeDtypeStruct((1, 5, *block), BF16)],
        in_specs=[pl.BlockSpec(memory_space=pl.ANY), v, v],
        out_specs=[pl.BlockSpec(memory_space=pl.ANY)],
        scratch_shapes=[pltpu.VMEM(block, BF16), pltpu.SemaphoreType.DMA],
        input_output_aliases={0: 0},
        cost_estimate=pl.CostEstimate(flops=size * size, bytes_accessed=1_000_000, transcendentals=0),
        compiler_params=pltpu.CompilerParams(vmem_limit_bytes=VMEM),
        name="finish",
    )(out, tail, c2)
    return out


def solution(mesh):
    in_specs = (
        P("site", None, "sector", None),
        P("site", None, "sector", None),
        P("site", None, None, None, None),
        P(None, "sector", None),
    )

    def body(*args):
        return local(mesh.shape["site"], mesh.shape["sector"], *args)

    return jax.shard_map(
        body, mesh=mesh, in_specs=in_specs, out_specs=P("site", None, "sector", None), check_vma=False
    )
```

```python
import jax
import jax.numpy as jnp
from jax import lax
from jax.experimental import pallas as pl
from jax.experimental.pallas import tpu as pltpu
from jax.sharding import PartitionSpec as P


BF16 = jnp.bfloat16
F32 = jnp.float32
AXES = ("site", "sector")
FLAT = (0, 3, 4)
ROWS = 128
VMEM = 16 * 2**20


def dot(a, b):
    return jnp.dot(a, b, preferred_element_type=F32)


def row_blocks(count):
    step = ROWS if count % ROWS == 0 else count
    return [slice(start, start + step) for start in range(0, count, step)]


def coupling(ref, w, v, s, t):
    return ref[w * 20 + v * 4 + s * 2 + t]


def whole():
    return pl.BlockSpec(memory_space=pltpu.VMEM)


def scalars():
    return pl.BlockSpec(memory_space=pltpu.SMEM)


def kernel_call(body, outs, flops, specs, scratch=(), place=pltpu.VMEM):
    return pl.pallas_call(
        body,
        out_shape=[jax.ShapeDtypeStruct(shape, kind) for shape, kind in outs],
        in_specs=specs,
        out_specs=[pl.BlockSpec(memory_space=place) for _ in outs],
        scratch_shapes=list(scratch),
        cost_estimate=pl.CostEstimate(flops=flops, bytes_accessed=4_000_000, transcendentals=0),
        compiler_params=pltpu.CompilerParams(vmem_limit_bytes=VMEM),
    )


def split(env, bnd, own, s34, s2, own_up):
    s34[...] = jnp.where(
        lax.axis_index("site") == lax.axis_size("site") - 1, bnd[3:5], env[3:5]
    )
    s2[...] = env[2:3]
    own_up[...] = own[0]


def early(k, bnd, arr10, own, e01, h01, z034, c2, own_t, y):
    h01[...] = arr10[...]
    e01[...] = jnp.where(lax.axis_index("site") == 0, bnd[0:2], arr10[...])
    own_t[0] = own[0].T
    own_t[1] = own[1].T
    y[...] = dot(e01[0], own[0])
    for r in row_blocks(y.shape[0]):
        for i, v in enumerate(FLAT):
            z034[i, r] = coupling(k, 0, v, 0, 0) * y[r]
        c2[r] = coupling(k, 0, 2, 1, 0) * y[r]


def middle(k, bnd, arr34, own, near, z034_in, c2_in, z034, c2, near_t, y):
    near_t[...] = near[1].T
    first = lax.axis_index("site") == 0
    y[0] = dot(jnp.where(first, bnd[3], arr34[0]), own[0])
    y[1] = dot(jnp.where(first, bnd[4], arr34[1]), own[0])
    for r in row_blocks(y.shape[1]):
        for i, v in enumerate(FLAT):
            z034[i, r] = (
                z034_in[i, r]
                + coupling(k, 3, v, 0, 0) * y[0, r]
                + coupling(k, 4, v, 0, 0) * y[1, r]
            )
        c2[r] = c2_in[r] + coupling(k, 3, 2, 1, 0) * y[0, r] + coupling(k, 4, 2, 1, 0) * y[1, r]


def send(k, bnd, arr2, near, own_t, c2_in, c2, y2):
    e2 = jnp.where(lax.axis_index("site") == 0, bnd[2], arr2[0])
    y2[...] = dot(e2, near[1])
    z = (c2_in[...] + coupling(k, 2, 2, 1, 1) * y2[...]).astype(BF16)
    c2[...] = dot(own_t[1], z).astype(BF16)


def late(k, bnd, e01, arr34, arr2, own, near, up, own_t, z034_in, y2, p0, last, p1):
    first = lax.axis_index("site") == 0
    e0 = e01[0].astype(F32)
    e3 = jnp.where(first, bnd[3], arr34[0]).astype(F32)
    e4 = jnp.where(first, bnd[4], arr34[1]).astype(F32)
    e034 = (
        coupling(k, 0, 1, 0, 1) * e0 + coupling(k, 3, 1, 0, 1) * e3 + coupling(k, 4, 1, 0, 1) * e4
    ).astype(BF16)
    y = dot(jnp.where(first, bnd[2], arr2[0]), near[0])
    last[...] = dot(own_t[0], (coupling(k, 2, 2, 0, 0) * y).astype(BF16))
    for i, v in enumerate(FLAT):
        z = (z034_in[i] + coupling(k, 2, v, 0, 1) * y2[...]).astype(BF16)
        p0[i] = dot(own_t[0], z)
    y = coupling(k, 1, 1, 0, 0) * dot(e01[1], up[...])
    p1[...] = dot(own_t[0], (dot(e034, own[1]) + y).astype(BF16))


def join(k, h01, got10, arr34, got34, own, near, near_t, p0, p1, out, y, done, sems):
    copies = []

    def store(v, total):
        i = len(copies)
        done[i] = total.astype(BF16)
        copies.append(pltpu.make_async_copy(done.at[i], out.at[0, v], sems.at[i]))
        copies[i].start()

    first = lax.axis_index("site") == 0
    f1 = jnp.where(first, h01[1], got10[1])
    y[0] = dot(jnp.where(first, h01[0], got10[0]), near[1])
    y[1] = dot(f1, own[0])
    carried = dot(near_t[...], (coupling(k, 1, 1, 1, 1) * dot(f1, own[1])).astype(BF16))
    store(1, p1[...] + carried.astype(BF16).astype(F32))
    y[2] = dot(jnp.where(first, arr34[0], got34[0]), near[1])
    y[3] = dot(jnp.where(first, arr34[1], got34[1]), near[1])
    for i, v in enumerate(FLAT):
        z = (
            coupling(k, 0, v, 1, 1) * y[0]
            + coupling(k, 1, v, 1, 0) * y[1]
            + coupling(k, 3, v, 1, 1) * y[2]
            + coupling(k, 4, v, 1, 1) * y[3]
        ).astype(BF16)
        store(v, p0[i] + dot(near_t[...], z).astype(BF16).astype(F32))
    for copy in copies:
        copy.wait()


def finish(out_in, p0, c2, out, buf, sem):
    buf[...] = (p0[...] + c2[...].astype(F32)).astype(BF16)
    copy = pltpu.make_async_copy(buf, out.at[0, 2], sem)
    copy.start()
    copy.wait()


def local(sites, sectors, site_tensors, environments, mpo, boundary):
    def pairs(move, starts):
        found = []
        for s in starts:
            for q in range(sectors):
                to, r = move(s, q)
                found.append((s * sectors + q, to * sectors + r % sectors))
        return found

    everywhere = range(sites)
    ahead = pairs(lambda s, q: (s, q + 1), everywhere)
    behind = pairs(lambda s, q: (s, q - 1), everywhere)
    inner = pairs(lambda s, q: (s, q + 1), range(1, sites))
    along = pairs(lambda s, q: (s + 1, q) if s + 1 < sites else (0, q + 1), everywhere)
    along_open = pairs(lambda s, q: (s + 1, q), range(sites - 1))

    own = site_tensors[0]
    env = environments[0]
    size = own.shape[-1]
    block = (size, size)
    flop = 2 * size**3
    k = mpo.reshape(-1)
    last = lax.axis_index("site") == sites - 1

    def send_on(value, route):
        return lax.ppermute(value, AXES, route)

    v = whole()
    arr10 = send_on(jnp.where(last, boundary[0:2], env[0:2]), along)
    s34, s2, own_up = kernel_call(
        split, [((2, *block), BF16), ((1, *block), BF16), (block, BF16)], size * size, [v] * 3
    )(env, boundary, own)
    near = send_on(own, ahead)
    arr34 = send_on(s34, along)
    up = send_on(own_up, behind)
    arr2 = send_on(s2, along_open)
    got10 = send_on(arr10, inner)

    e01, h01, z034, c2, own_t = kernel_call(
        early,
        [((2, *block), BF16), ((2, *block), BF16), ((3, *block), F32), (block, F32), ((2, *block), BF16)],
        flop,
        [scalars()] + [v] * 3,
        [pltpu.VMEM(block, F32)],
    )(k, boundary, arr10, own)
    got34 = send_on(arr34, inner)
    z034, c2, near_t = kernel_call(
        middle,
        [((3, *block), F32), (block, F32), (block, BF16)],
        2 * flop,
        [scalars()] + [v] * 6,
        [pltpu.VMEM((2, *block), F32)],
    )(k, boundary, arr34, own, near, z034, c2)
    c2, y2 = kernel_call(
        send, [(block, BF16), (block, F32)], 2 * flop, [scalars()] + [v] * 5
    )(k, boundary, arr2, near, own_t, c2)
    c2 = send_on(c2, ahead)
    p0, tail, p1 = kernel_call(
        late, [((3, *block), F32), (block, F32), (block, F32)], 8 * flop, [scalars()] + [v] * 10
    )(k, boundary, e01, arr34, arr2, own, near, up, own_t, z034, y2)
    (out,) = kernel_call(
        join,
        [((1, 5, *block), BF16)],
        9 * flop,
        [scalars()] + [v] * 9,
        [
            pltpu.VMEM((4, *block), F32),
            pltpu.VMEM((4, *block), BF16),
            pltpu.SemaphoreType.DMA((4,)),
        ],
        place=pltpu.HBM,
    )(k, h01, got10, arr34, got34, own, near, near_t, p0, p1)
    (out,) = pl.pallas_call(
        finish,
        out_shape=[jax.ShapeDtypeStruct((1, 5, *block), BF16)],
        in_specs=[pl.BlockSpec(memory_space=pl.ANY), v, v],
        out_specs=[pl.BlockSpec(memory_space=pl.ANY)],
        scratch_shapes=[pltpu.VMEM(block, BF16), pltpu.SemaphoreType.DMA],
        input_output_aliases={0: 0},
        cost_estimate=pl.CostEstimate(flops=size * size, bytes_accessed=1_000_000, transcendentals=0),
        compiler_params=pltpu.CompilerParams(vmem_limit_bytes=VMEM),
        name="finish",
    )(out, tail, c2)
    return out


def solution(mesh):
    in_specs = (
        P("site", None, "sector", None),
        P("site", None, "sector", None),
        P("site", None, None, None, None),
        P(None, "sector", None),
    )

    def body(*args):
        return local(mesh.shape["site"], mesh.shape["sector"], *args)

    return jax.shard_map(
        body, mesh=mesh, in_specs=in_specs, out_specs=P("site", None, "sector", None), check_vma=False
    )
```

```python
import jax
import jax.numpy as jnp
from jax import lax
from jax.experimental import pallas as pl
from jax.experimental.pallas import tpu as pltpu
from jax.sharding import PartitionSpec as P


BF16 = jnp.bfloat16
F32 = jnp.float32
AXES = ("site", "sector")
FLAT = (0, 3, 4)
ROWS = 128
VMEM = 16 * 2**20


def dot(a, b):
    return jnp.dot(a, b, preferred_element_type=F32)


def row_blocks(count):
    step = ROWS if count % ROWS == 0 else count
    return [slice(start, start + step) for start in range(0, count, step)]


def coupling(ref, w, v, s, t):
    return ref[w * 20 + v * 4 + s * 2 + t]


def whole():
    return pl.BlockSpec(memory_space=pltpu.VMEM)


def scalars():
    return pl.BlockSpec(memory_space=pltpu.SMEM)


def kernel_call(body, outs, flops, specs, scratch=(), place=pltpu.VMEM):
    return pl.pallas_call(
        body,
        out_shape=[jax.ShapeDtypeStruct(shape, kind) for shape, kind in outs],
        in_specs=specs,
        out_specs=[pl.BlockSpec(memory_space=place) for _ in outs],
        scratch_shapes=list(scratch),
        cost_estimate=pl.CostEstimate(flops=flops, bytes_accessed=4_000_000, transcendentals=0),
        compiler_params=pltpu.CompilerParams(vmem_limit_bytes=VMEM),
    )


def split(env, bnd, own, s34, s2, own_up):
    s34[...] = jnp.where(
        lax.axis_index("site") == lax.axis_size("site") - 1, bnd[3:5], env[3:5]
    )
    s2[...] = env[2:3]
    own_up[...] = own[0]


def early(k, bnd, arr10, own, e01, h01, z034, c2, own_t, y):
    h01[...] = arr10[...]
    e01[...] = jnp.where(lax.axis_index("site") == 0, bnd[0:2], arr10[...])
    own_t[0] = own[0].T
    own_t[1] = own[1].T
    y[...] = dot(e01[0], own[0])
    for r in row_blocks(y.shape[0]):
        for i, v in enumerate(FLAT):
            z034[i, r] = coupling(k, 0, v, 0, 0) * y[r]
        c2[r] = coupling(k, 0, 2, 1, 0) * y[r]


def middle(k, bnd, arr34, own, near, z034_in, c2_in, z034, c2, near_t, y):
    near_t[...] = near[1].T
    first = lax.axis_index("site") == 0
    y[0] = dot(jnp.where(first, bnd[3], arr34[0]), own[0])
    y[1] = dot(jnp.where(first, bnd[4], arr34[1]), own[0])
    for r in row_blocks(y.shape[1]):
        for i, v in enumerate(FLAT):
            z034[i, r] = (
                z034_in[i, r]
                + coupling(k, 3, v, 0, 0) * y[0, r]
                + coupling(k, 4, v, 0, 0) * y[1, r]
            )
        c2[r] = c2_in[r] + coupling(k, 3, 2, 1, 0) * y[0, r] + coupling(k, 4, 2, 1, 0) * y[1, r]


def send(k, bnd, arr2, near, own_t, c2_in, c2, y2):
    e2 = jnp.where(lax.axis_index("site") == 0, bnd[2], arr2[0])
    y2[...] = dot(e2, near[1])
    z = (c2_in[...] + coupling(k, 2, 2, 1, 1) * y2[...]).astype(BF16)
    c2[...] = dot(own_t[1], z).astype(BF16)


def late(k, bnd, e01, arr34, arr2, own, near, own_t, z034_in, y2, p0, last, z1):
    first = lax.axis_index("site") == 0
    e0 = e01[0].astype(F32)
    e3 = jnp.where(first, bnd[3], arr34[0]).astype(F32)
    e4 = jnp.where(first, bnd[4], arr34[1]).astype(F32)
    e034 = (
        coupling(k, 0, 1, 0, 1) * e0 + coupling(k, 3, 1, 0, 1) * e3 + coupling(k, 4, 1, 0, 1) * e4
    ).astype(BF16)
    y = dot(jnp.where(first, bnd[2], arr2[0]), near[0])
    last[...] = dot(own_t[0], (coupling(k, 2, 2, 0, 0) * y).astype(BF16))
    for i, v in enumerate(FLAT):
        z = (z034_in[i] + coupling(k, 2, v, 0, 1) * y2[...]).astype(BF16)
        p0[i] = dot(own_t[0], z)
    z1[...] = dot(e034, own[1])


def join(k, h01, got10, arr34, got34, e01, up, own, own_t, near, near_t, p0, z1, out, y, done, sems):
    copies = []

    def store(v, total):
        i = len(copies)
        done[i] = total.astype(BF16)
        copies.append(pltpu.make_async_copy(done.at[i], out.at[0, v], sems.at[i]))
        copies[i].start()

    first = lax.axis_index("site") == 0
    f1 = jnp.where(first, h01[1], got10[1])
    y[0] = dot(jnp.where(first, h01[0], got10[0]), near[1])
    y[1] = dot(f1, own[0])
    carried = dot(near_t[...], (coupling(k, 1, 1, 1, 1) * dot(f1, own[1])).astype(BF16))
    z = z1[...] + coupling(k, 1, 1, 0, 0) * dot(e01[1], up[...])
    store(1, dot(own_t[0], z.astype(BF16)) + carried.astype(BF16).astype(F32))
    y[2] = dot(jnp.where(first, arr34[0], got34[0]), near[1])
    y[3] = dot(jnp.where(first, arr34[1], got34[1]), near[1])
    for i, v in enumerate(FLAT):
        z = (
            coupling(k, 0, v, 1, 1) * y[0]
            + coupling(k, 1, v, 1, 0) * y[1]
            + coupling(k, 3, v, 1, 1) * y[2]
            + coupling(k, 4, v, 1, 1) * y[3]
        ).astype(BF16)
        store(v, p0[i] + dot(near_t[...], z).astype(BF16).astype(F32))
    for copy in copies:
        copy.wait()


def finish(out_in, p0, c2, out, buf, sem):
    buf[...] = (p0[...] + c2[...].astype(F32)).astype(BF16)
    copy = pltpu.make_async_copy(buf, out.at[0, 2], sem)
    copy.start()
    copy.wait()


def local(sites, sectors, site_tensors, environments, mpo, boundary):
    def pairs(move, starts):
        found = []
        for s in starts:
            for q in range(sectors):
                to, r = move(s, q)
                found.append((s * sectors + q, to * sectors + r % sectors))
        return found

    everywhere = range(sites)
    ahead = pairs(lambda s, q: (s, q + 1), everywhere)
    behind = pairs(lambda s, q: (s, q - 1), everywhere)
    inner = pairs(lambda s, q: (s, q + 1), range(1, sites))
    along = pairs(lambda s, q: (s + 1, q) if s + 1 < sites else (0, q + 1), everywhere)
    along_open = pairs(lambda s, q: (s + 1, q), range(sites - 1))

    own = site_tensors[0]
    env = environments[0]
    size = own.shape[-1]
    block = (size, size)
    flop = 2 * size**3
    k = mpo.reshape(-1)
    last = lax.axis_index("site") == sites - 1

    def send_on(value, route):
        return lax.ppermute(value, AXES, route)

    v = whole()
    arr10 = send_on(jnp.where(last, boundary[0:2], env[0:2]), along)
    s34, s2, own_up = kernel_call(
        split, [((2, *block), BF16), ((1, *block), BF16), (block, BF16)], size * size, [v] * 3
    )(env, boundary, own)
    near = send_on(own, ahead)
    arr34 = send_on(s34, along)
    up = send_on(own_up, behind)
    arr2 = send_on(s2, along_open)
    got10 = send_on(arr10, inner)

    e01, h01, z034, c2, own_t = kernel_call(
        early,
        [((2, *block), BF16), ((2, *block), BF16), ((3, *block), F32), (block, F32), ((2, *block), BF16)],
        flop,
        [scalars()] + [v] * 3,
        [pltpu.VMEM(block, F32)],
    )(k, boundary, arr10, own)
    got34 = send_on(arr34, inner)
    z034, c2, near_t = kernel_call(
        middle,
        [((3, *block), F32), (block, F32), (block, BF16)],
        2 * flop,
        [scalars()] + [v] * 6,
        [pltpu.VMEM((2, *block), F32)],
    )(k, boundary, arr34, own, near, z034, c2)
    c2, y2 = kernel_call(
        send, [(block, BF16), (block, F32)], 2 * flop, [scalars()] + [v] * 5
    )(k, boundary, arr2, near, own_t, c2)
    c2 = send_on(c2, ahead)
    p0, tail, z1 = kernel_call(
        late, [((3, *block), F32), (block, F32), (block, F32)], 6 * flop, [scalars()] + [v] * 9
    )(k, boundary, e01, arr34, arr2, own, near, own_t, z034, y2)
    (out,) = kernel_call(
        join,
        [((1, 5, *block), BF16)],
        11 * flop,
        [scalars()] + [v] * 12,
        [
            pltpu.VMEM((4, *block), F32),
            pltpu.VMEM((4, *block), BF16),
            pltpu.SemaphoreType.DMA((4,)),
        ],
        place=pltpu.HBM,
    )(k, h01, got10, arr34, got34, e01, up, own, own_t, near, near_t, p0, z1)
    (out,) = pl.pallas_call(
        finish,
        out_shape=[jax.ShapeDtypeStruct((1, 5, *block), BF16)],
        in_specs=[pl.BlockSpec(memory_space=pl.ANY), v, v],
        out_specs=[pl.BlockSpec(memory_space=pl.ANY)],
        scratch_shapes=[pltpu.VMEM(block, BF16), pltpu.SemaphoreType.DMA],
        input_output_aliases={0: 0},
        cost_estimate=pl.CostEstimate(flops=size * size, bytes_accessed=1_000_000, transcendentals=0),
        compiler_params=pltpu.CompilerParams(vmem_limit_bytes=VMEM),
        name="finish",
    )(out, tail, c2)
    return out


def solution(mesh):
    in_specs = (
        P("site", None, "sector", None),
        P("site", None, "sector", None),
        P("site", None, None, None, None),
        P(None, "sector", None),
    )

    def body(*args):
        return local(mesh.shape["site"], mesh.shape["sector"], *args)

    return jax.shard_map(
        body, mesh=mesh, in_specs=in_specs, out_specs=P("site", None, "sector", None), check_vma=False
    )
```
